32 devices in a mesh: row: 4 (over y, core), col: 8 (over z, x).
Axes of the slice: x: 2, y: 2, z: 4, core: 2. Of those that a mesh axis runs over, the one named last changes fastest.
Arguments:
- features: bfloat16 [8192, 512], P(('col', 'row')), may hold values from -6 to 6
- positions: float32 [3, 8192], replicated, may hold values from 0 to 20, as said below
- cluster_atoms: int32 [64], replicated, may hold values from 64 to 128, as said below
- pair_cells: int32 [4, 8, 12], P('row', 'col'), may hold values from 0 to 127, as said below
- pair_count: int32 [4, 8], P('row', 'col'), may hold values from 1 to 12, as said below
- project_weight: bfloat16 [512, 512], replicated, may hold values from -0.25 to 0.25
- basis_filter: float32 [16, 512], replicated, may hold values from -0.375 to 0.375
- hidden_weight: bfloat16 [512, 512], replicated, may hold values from -0.25 to 0.25
- hidden_bias: float32 [512], replicated, may hold values from -4 to 4
- output_weight: bfloat16 [512, 512], replicated, may hold values from -0.25 to 0.25
- output_bias: float32 [512], replicated, may hold values from -3 to 3
Outputs:
- update: bfloat16 [8192, 512], P('row')
The draws below stay inside these ranges and needn't reach their ends.
Inputs may be any that keep to these rules, and one draw needn't show every extreme that they name: `positions`: each cluster's atoms lie in a cube of side 5 of its own. `cluster_atoms`: atoms of a cluster at slots below the count are real, the others padding; some cluster is full. `pair_cells`: entry v names target cluster v // 8 of the row's block of 16 clusters and source cluster v mod 8 of the column's block of 8 clusters; the entries of one device are distinct; only the first pair_count entries are used. `pair_count`: some device lists 12 pairs.
All inputs are finite; a program needn't handle non-finite values.
Results may differ from the reference program's by a relative error of at most 0.0048.
Values may be sent and summed in bfloat16 or wider, within the bound.
No kernel may reach another device: no remote copies, remote signals or barrier semaphores. Data moves between devices by JAX's collectives and lax.ppermute only.
A program may use at most 64 MiB of HBM per device.

```python
import math
import jax
import jax.numpy as jnp
from jax import lax

CL = 128
F = 512
NRBF = 16
CPR = 16
PCAP = 12
SPC = 8
NCLUS = 64
NATOM = 8192
N_ROW = 4
N_COL = 8


cell_side = 5.0


def cluster_layout(key):
    order = jax.random.permutation(jax.random.fold_in(key, 5), NCLUS).astype(jnp.int32)
    cell_x = order % 4
    cell_y = order // 4 % 4
    cell_z = order // 16
    return jnp.stack([cell_x, cell_y, cell_z]).astype(jnp.int32)


def pair_layout(key):
    cells = cluster_layout(key)
    candidates = CPR * SPC
    rows = jnp.arange(N_ROW, dtype=jnp.int32)[:, None, None]
    cols = jnp.arange(N_COL, dtype=jnp.int32)[None, :, None]
    entries = jnp.arange(candidates, dtype=jnp.int32)[None, None, :]
    target = rows * CPR + entries // SPC
    source = cols * SPC + entries % SPC
    target = jnp.broadcast_to(target, (N_ROW, N_COL, candidates))
    source = jnp.broadcast_to(source, (N_ROW, N_COL, candidates))
    gap = jnp.max(jnp.abs(cells[:, target] - cells[:, source]), axis=0)
    nearness = jnp.minimum(gap, 2)
    device_keys = jax.random.split(jax.random.fold_in(key, 23), N_ROW * N_COL)
    ties = jax.vmap(lambda single: jax.random.permutation(single, candidates))(device_keys)
    ties = ties.reshape(N_ROW, N_COL, candidates).astype(jnp.int32)
    score = nearness * candidates + ties
    ranked = jnp.argsort(score, axis=-1, stable=True).astype(jnp.int32)
    listed_cells = ranked[:, :, :PCAP]
    adjacent = jnp.sum((gap <= 1).astype(jnp.int32), axis=-1)
    listed = jnp.clip(adjacent, 1, PCAP).reshape(-1)
    chosen = jax.random.randint(jax.random.fold_in(key, 37), (), 0, N_ROW * N_COL)
    listed = jnp.where(jnp.arange(N_ROW * N_COL) == chosen, PCAP, listed)
    return (listed_cells.astype(jnp.int32), listed.reshape(N_ROW, N_COL).astype(jnp.int32))


def draw_positions(key, part):
    cells = cluster_layout(key).astype(jnp.float32) * cell_side
    corners = jnp.repeat(cells, CL, axis=1)
    inside = jax.random.uniform(jax.random.fold_in(key, 7), (3, NATOM), jnp.float32, 0.0, cell_side)
    return (corners + inside).astype(jnp.float32)


def draw_cluster_atoms(key, part):
    count_key, pick_key = jax.random.split(jax.random.fold_in(key, 11))
    counts = jax.random.randint(count_key, (NCLUS,), CL // 2, CL + 1)
    chosen = jax.random.randint(pick_key, (), 0, NCLUS)
    return jnp.where(jnp.arange(NCLUS) == chosen, CL, counts).astype(jnp.int32)


def draw_pair_cells(key, part):
    return pair_layout(key)[0]


def draw_pair_count(key, part):
    return pair_layout(key)[1]


def block_levels(own_key, dims, cuts, smallest, largest):
    loudness = 1.0
    for position, parts in cuts:
        steps = jax.random.uniform(jax.random.fold_in(jax.random.fold_in(own_key, 6), position), (parts,), jnp.float32, smallest / len(cuts), largest / len(cuts))
        loudness = loudness * jnp.repeat(jnp.exp(steps), dims[position] // parts).reshape((-1,) + (1,) * (len(dims) - 1 - position))
    return loudness


def gaussian(rng, shape, deviation, bound, cuts=(), kind=jnp.bfloat16):
    values = deviation * jax.random.normal(rng, shape, jnp.float32)
    if cuts:
        values = values * block_levels(rng, shape, cuts, -0.22, 0.18)
    return jnp.clip(values, -bound, bound).astype(kind)


def setup_inputs(seed: int = 0) -> dict:
    key_of = jax.random.split(jax.random.key(seed), 12)
    features = gaussian(key_of[0], (NATOM, F), 1.0, 6.0, ((0, 32),))
    positions = draw_positions(jax.random.fold_in(key_of[11], 71), 0)
    cluster_atoms = draw_cluster_atoms(jax.random.fold_in(key_of[11], 71), 0)
    pair_cells = draw_pair_cells(jax.random.fold_in(key_of[11], 71), 0)
    pair_count = draw_pair_count(jax.random.fold_in(key_of[11], 71), 0)
    project_weight = gaussian(key_of[5], (F, F), F ** -0.5, 0.25)
    basis_filter = gaussian(key_of[6], (NRBF, F), (2 * CL) ** -0.5, 0.375, (), jnp.float32)
    hidden_weight = gaussian(key_of[7], (F, F), F ** -0.5, 0.25)
    hidden_bias = gaussian(key_of[8], (F,), 1.0, 4.0, (), jnp.float32)
    output_weight = gaussian(key_of[9], (F, F), F ** -0.5, 0.25)
    output_bias = gaussian(key_of[10], (F,), 0.5, 3.0, (), jnp.float32)
    return dict(features=features, positions=positions, cluster_atoms=cluster_atoms, pair_cells=pair_cells, pair_count=pair_count, project_weight=project_weight, basis_filter=basis_filter, hidden_weight=hidden_weight, hidden_bias=hidden_bias, output_weight=output_weight, output_bias=output_bias)


cutoff_radius = 5.0

def basis_weights(target_pos, source_pos, target_first, source_first, source_valid, basis_count):
    cluster = target_pos.shape[1]
    squared = jnp.zeros((cluster, cluster), jnp.float32)
    for component in range(3):
        difference = target_pos[component][:, None] - source_pos[component][None, :]
        squared = squared + difference * difference
    distance = jnp.sqrt(squared)
    target_ids = target_first + lax.broadcasted_iota(jnp.int32, (cluster, cluster), 0)
    source_local = lax.broadcasted_iota(jnp.int32, (cluster, cluster), 1)
    allowed = (target_ids != source_first + source_local) & (source_local < source_valid) & (distance < cutoff_radius)
    smooth = 0.5 * (jnp.cos(math.pi / cutoff_radius * distance) + 1.0)
    envelope = jnp.where(allowed, smooth, 0.0)
    centers = lax.broadcasted_iota(jnp.int32, (1, basis_count, 1), 1).astype(jnp.float32) * (cutoff_radius / (basis_count - 1))
    sharpness = ((basis_count - 1) / cutoff_radius) ** 2
    offset = distance[:, None, :] - centers
    weights = jnp.exp(-sharpness * offset * offset) * envelope[:, None, :]
    return weights.astype(jnp.bfloat16).reshape(cluster, basis_count * cluster)

def scaled_sources(source_rows, basis_filter):
    scaled = basis_filter[:, None, :] * source_rows[None, :, :].astype(jnp.float32)
    return scaled.astype(jnp.bfloat16).reshape(-1, source_rows.shape[1])

def refine(message, first_atom, cluster_atoms, hidden_weight, hidden_bias, output_weight, output_bias, cluster):
    rounded = message.astype(jnp.bfloat16)
    hidden = jnp.dot(rounded, hidden_weight, preferred_element_type=jnp.float32) + hidden_bias
    hidden = (jax.nn.softplus(hidden) - math.log(2.0)).astype(jnp.bfloat16)
    result = jnp.dot(hidden, output_weight, preferred_element_type=jnp.float32) + output_bias
    row_total = message.shape[0]
    atom_ids = first_atom + lax.broadcasted_iota(jnp.int32, (row_total, 1), 0)
    cluster_ids = atom_ids // cluster
    table_ids = lax.broadcasted_iota(jnp.int32, (1, cluster_atoms.shape[0]), 1)
    valid_atoms = lax.optimization_barrier(jnp.sum(jnp.where(cluster_ids == table_ids, cluster_atoms[None, :], 0), axis=1, keepdims=True))
    keeping = atom_ids - cluster_ids * cluster < valid_atoms
    return jnp.where(keeping, result, 0.0).astype(jnp.bfloat16)

def reference(features, positions, cluster_atoms, pair_cells, pair_count, project_weight, basis_filter, hidden_weight, hidden_bias, output_weight, output_bias):
    projected = jnp.dot(features, project_weight, preferred_element_type=jnp.float32).astype(jnp.bfloat16)
    messages = jnp.zeros((positions.shape[1], F), jnp.float32)

    def device_step(device, running_all):
        device_id = jnp.asarray(device).astype(jnp.int32)
        row_index = device_id // N_COL
        col_index = device_id - row_index * N_COL
        listed = pair_count[row_index, col_index]

        def add_pair(slot_index, running):
            pair_cell = pair_cells[row_index, col_index, slot_index]
            target_local = pair_cell // SPC
            source_local = pair_cell - target_local * SPC
            target_first = ((row_index * CPR + target_local) * CL).astype(jnp.int32)
            source_cluster = (col_index * SPC + source_local).astype(jnp.int32)
            source_first = (source_cluster * CL).astype(jnp.int32)
            target_pos = lax.dynamic_slice_in_dim(positions, target_first, CL, 1)
            source_pos = lax.dynamic_slice_in_dim(positions, source_first, CL, 1)
            source_valid = cluster_atoms[source_cluster]
            weights = basis_weights(target_pos, source_pos, target_first, source_first, source_valid, NRBF)
            source_rows = lax.dynamic_slice_in_dim(projected, source_first, CL, 0)
            message = jnp.dot(weights, scaled_sources(source_rows, basis_filter), preferred_element_type=jnp.float32)
            current = lax.dynamic_slice_in_dim(running, target_first, CL, 0)
            return lax.dynamic_update_slice_in_dim(running, current + message, target_first, 0)
        return lax.fori_loop(0, listed, add_pair, running_all)
    messages = lax.fori_loop(0, N_ROW * N_COL, device_step, messages)
    return refine(messages, 0, cluster_atoms, hidden_weight, hidden_bias, output_weight, output_bias, CL)
```

```python
import functools
import math

import jax
import jax.numpy as jnp
from jax import lax
from jax.experimental import pallas as pl
from jax.experimental.pallas import tpu as pltpu
from jax.sharding import PartitionSpec as P

CL = 128
CPR = 16
CUTOFF = 5.0
MIB = 1 << 20

SMEM = pl.BlockSpec(memory_space=pltpu.SMEM)
VMEM = pl.BlockSpec(memory_space=pltpu.VMEM)


def basis_kernel(cells, count, place, atoms, positions, out, *, sources, rbf):
    step = CUTOFF / (rbf - 1)
    sharp = 1.0 / step**2
    middle = rbf // 2
    slope = 2.0 * sharp * step
    shrink = math.exp(-2.0 * sharp * step * step)
    row_lane = lax.broadcasted_iota(jnp.int32, (CL, CL), 1)
    row_sub = lax.broadcasted_iota(jnp.int32, (CL, CL), 0)

    def pair(slot, carry):
        cell = cells[slot]
        target = lax.div(cell, sources)
        source = place[1] + cell - target * sources
        target = place[0] + target
        at_target = pl.ds(pl.multiple_of(target * CL, CL), CL)
        at_source = pl.ds(pl.multiple_of(source * CL, CL), CL)
        squared = jnp.zeros((CL, CL), jnp.float32)
        for component in range(3):
            across = jnp.broadcast_to(positions[component : component + 1, at_target], (CL, CL))
            along = positions[component : component + 1, at_source]
            difference = jnp.transpose(across) - along
            squared = squared + difference * difference
        distance = jnp.sqrt(squared)
        itself = (row_sub == row_lane) & (target == source)
        allowed = (row_lane < atoms[source]) & (distance < CUTOFF) & jnp.logical_not(itself)
        smooth = 0.5 * (jnp.cos(math.pi / CUTOFF * distance) + 1.0)
        envelope = jnp.where(allowed, smooth, 0.0)
        inside = jnp.minimum(distance, CUTOFF)
        offset = inside - middle * step
        start = jnp.exp(-sharp * offset * offset) * envelope
        out[slot, middle * CL : (middle + 1) * CL, :] = start.astype(out.dtype)
        value, ratio = start, jnp.exp(slope * offset - sharp * step * step)
        for k in range(middle + 1, rbf):
            value = value * ratio
            out[slot, k * CL : (k + 1) * CL, :] = value.astype(out.dtype)
            ratio = ratio * shrink
        value, ratio = start, jnp.exp(-slope * offset - sharp * step * step)
        for k in range(middle - 1, -1, -1):
            value = value * ratio
            out[slot, k * CL : (k + 1) * CL, :] = value.astype(out.dtype)
            ratio = ratio * shrink
        return carry

    lax.fori_loop(0, count[0], pair, 0)


def basis_of(cells, count, place, atoms, positions, sources, rbf):
    return pl.pallas_call(
        functools.partial(basis_kernel, sources=sources, rbf=rbf),
        out_shape=jax.ShapeDtypeStruct((cells.shape[0], rbf * CL, CL), jnp.bfloat16),
        in_specs=[SMEM, SMEM, SMEM, SMEM, VMEM],
        out_specs=VMEM,
        compiler_params=pltpu.CompilerParams(vmem_limit_bytes=16 * MIB),
        name="pair_basis",
    )(cells, count, place, atoms, positions)


def message_kernel(cells, count, row_of, slot_of, basis, basis_filter, *rest, sources, send_rows, unit, rbf):
    pieces, (send, keep, rows, total) = rest[:-4], rest[-4:]
    depth = pieces[0].shape[0]
    for n, piece in enumerate(pieces):
        at = pl.multiple_of(slot_of[n] * depth, 16)
        rows[pl.ds(at, depth), :] = piece[...]
    total[...] = jnp.zeros_like(total)

    def pair(slot, carry):
        cell = cells[slot]
        target = lax.div(cell, sources)
        source = cell - target * sources
        places = [row_of[target * (CL // unit) + n] for n in range(CL // unit)]

        @pl.when(functools.reduce(jnp.maximum, places) >= 0)
        def _():
            there = pl.ds(pl.multiple_of(source * CL, CL), CL)
            projected = rows[there, :].astype(jnp.float32)
            scaled = jnp.concatenate(
                [
                    (basis_filter[k : k + 1, :] * projected).astype(jnp.bfloat16)
                    for k in range(rbf)
                ],
                axis=0,
            )
            weights = jnp.concatenate(
                [basis[slot, k * CL : (k + 1) * CL, :] for k in range(rbf)], axis=1
            )
            found = jnp.dot(weights, scaled, preferred_element_type=jnp.float32)
            for n, first in enumerate(places):

                @pl.when(first >= 0)
                def _():
                    at = pl.ds(pl.multiple_of(first, unit), unit)
                    total[at, :] += found[n * unit : (n + 1) * unit]

        return carry

    lax.fori_loop(0, count[0], pair, 0)
    send[...] = total[:send_rows, :].astype(send.dtype)
    keep[...] = total[send_rows:, :]


def messages_of(cells, count, row_of, slot_of, basis, basis_filter, pieces, sources, group_rows, unit):
    channels = pieces[0].shape[1]
    rbf = basis_filter.shape[0]
    return pl.pallas_call(
        functools.partial(message_kernel, sources=sources, send_rows=group_rows, unit=unit, rbf=rbf),
        out_shape=(
            jax.ShapeDtypeStruct((group_rows, channels), jnp.bfloat16),
            jax.ShapeDtypeStruct((group_rows, channels), jnp.float32),
        ),
        in_specs=[SMEM] * 4 + [VMEM] * (2 + len(pieces)),
        out_specs=(VMEM, VMEM),
        scratch_shapes=[
            pltpu.VMEM((sources * CL, channels), jnp.bfloat16),
            pltpu.VMEM((2 * group_rows, channels), jnp.float32),
        ],
        compiler_params=pltpu.CompilerParams(vmem_limit_bytes=28 * MIB),
        name="pair_messages",
    )(cells, count, row_of, slot_of, basis, basis_filter, *pieces)


def refine_kernel(valid, hidden_weight, hidden_bias, output_weight, output_bias, kept, *rest):
    parts, out = rest[:-1], rest[-1]
    message = kept[...]
    for part in parts:
        message = message + part[...].astype(jnp.float32)
    rounded = message.astype(jnp.bfloat16)
    hidden = jnp.dot(rounded, hidden_weight[...], preferred_element_type=jnp.float32)
    hidden = hidden + hidden_bias[...]
    soft = jnp.maximum(hidden, 0.0) + jnp.log1p(jnp.exp(-jnp.abs(hidden)))
    hidden = (soft - math.log(2.0)).astype(jnp.bfloat16)
    result = jnp.dot(hidden, output_weight[...], preferred_element_type=jnp.float32)
    result = result + output_bias[...]
    unit = out.shape[0] // valid.shape[0]
    for n in range(valid.shape[0]):
        at = slice(n * unit, (n + 1) * unit)
        keeping = lax.broadcasted_iota(jnp.int32, (unit, out.shape[1]), 0) < valid[n]
        out[at, :] = jnp.where(keeping, result[at, :], 0.0).astype(out.dtype)


def refine(valid, hidden_weight, hidden_bias, output_weight, output_bias, kept, parts):
    return pl.pallas_call(
        refine_kernel,
        out_shape=jax.ShapeDtypeStruct(kept.shape, jnp.bfloat16),
        in_specs=[SMEM] + [VMEM] * (5 + len(parts)),
        out_specs=VMEM,
        compiler_params=pltpu.CompilerParams(vmem_limit_bytes=24 * MIB),
        name="update_rows",
    )(valid, hidden_weight, hidden_bias[None], output_weight, output_bias[None], kept, *parts)


def local(
    features,
    positions,
    cluster_atoms,
    pair_cells,
    pair_count,
    project_weight,
    basis_filter,
    hidden_weight,
    hidden_bias,
    output_weight,
    output_bias,
):
    row_total, col_total = lax.axis_size("row"), lax.axis_size("col")
    row_index, col_index = lax.axis_index("row"), lax.axis_index("col")
    row_outer, col_outer = row_total // 2, col_total // 2
    sources = features.shape[0] * row_total // CL
    own_rows = CPR * CL // col_total
    rbf = basis_filter.shape[0]

    def shift(value, axis, total, by):
        outer = total // 2
        pairs = [(2 * o + i, 2 * ((o + by) % outer) + i) for o in range(outer) for i in range(2)]
        return lax.ppermute(value, axis, pairs)

    def swap(value, axis, total):
        return lax.ppermute(value, axis, [(n, n ^ 1) for n in range(total)])

    cells, count = pair_cells[0, 0], pair_count[0]
    place = jnp.stack([row_index * CPR, col_index * sources]).astype(jnp.int32)

    projected = jnp.dot(features, project_weight, preferred_element_type=jnp.float32)
    projected = projected.astype(jnp.bfloat16)
    near = [projected] + [shift(projected, "row", row_total, by) for by in range(1, row_outer)]
    far = [swap(piece, "row", row_total) for piece in near]
    pieces = near + far
    outer, inner = row_index // 2, row_index % 2
    slot_of = jnp.stack(
        [((outer - by) % row_outer) * 2 + inner for by in range(row_outer)]
        + [((outer - by) % row_outer) * 2 + 1 - inner for by in range(row_outer)]
    ).astype(jnp.int32)
    basis = basis_of(cells, count, place, cluster_atoms, positions, sources, rbf)

    col_o, col_i = col_index // 2, col_index % 2
    half = col_outer // 2
    groups = [[half], [by for by in range(1, col_outer) if by != half], [0]]
    unit = min(own_rows, CL)
    unit_row = jnp.arange(CPR * CL // unit, dtype=jnp.int32) * unit
    owner = unit_row // own_rows
    owner_o, owner_i = owner // 2, owner % 2
    arrived = []
    kept_own = None
    for group in groups:
        relative = (owner_o - col_o) % col_outer
        row_of = jnp.full(owner.shape, -1, jnp.int32)
        for n, by in enumerate(group):
            first = jnp.where(owner_i == col_i, len(group) * own_rows, 0)
            first = first + n * own_rows + (unit_row - owner * own_rows)
            row_of = jnp.where(relative == by, first, row_of)
        send, keep = messages_of(
            cells, count, row_of, slot_of, basis, basis_filter, pieces, sources,
            len(group) * own_rows, unit,
        )
        received = swap(send, "col", col_total)
        if group == [0]:
            kept_own = keep
            arrived.append(received)
        else:
            summed = (keep + received.astype(jnp.float32)).astype(jnp.bfloat16)
            for n, by in enumerate(group):
                part = summed[n * own_rows : (n + 1) * own_rows]
                arrived.append(shift(part, "col", col_total, by))

    first_atom = row_index * (CPR * CL) + col_index * own_rows
    starts = first_atom + jnp.arange(own_rows // unit, dtype=jnp.int32) * unit
    valid = cluster_atoms[starts // CL] - starts % CL
    mine = refine(
        valid, hidden_weight, hidden_bias, output_weight, output_bias, kept_own, arrived
    )

    order = [by for by in range(1, col_outer) if by != half] + [half]
    found = {(0, 0): mine, (0, 1): swap(mine, "col", col_total)}
    for by in order:
        found[by, 0] = shift(mine, "col", col_total, by)
    for by in order:
        found[by, 1] = swap(found[by, 0], "col", col_total)
    result = jnp.zeros((CPR * CL, mine.shape[1]), mine.dtype)
    for (by, other), piece in found.items():
        from_o = (col_o - by) % col_outer
        from_i = 1 - col_i if other else col_i
        first = (from_o * 2 + from_i) * own_rows
        result = lax.dynamic_update_slice_in_dim(result, piece, first, 0)
    return result


def solution(mesh):
    in_specs = (
        P(("col", "row"), None),
        P(),
        P(),
        P("row", "col", None),
        P("row", "col"),
        P(),
        P(),
        P(),
        P(),
        P(),
        P(),
    )
    out_specs = P("row", None)
    return jax.shard_map(local, mesh=mesh, in_specs=in_specs, out_specs=out_specs, check_vma=False)
```

```python
import functools
import math

import jax
import jax.numpy as jnp
from jax import lax
from jax.experimental import pallas as pl
from jax.experimental.pallas import tpu as pltpu
from jax.sharding import PartitionSpec as P


CL = 128
CPR = 16
CUTOFF = 5.0
MIB = 1 << 20

SMEM = pl.BlockSpec(memory_space=pltpu.SMEM)
VMEM = pl.BlockSpec(memory_space=pltpu.VMEM)


def basis_kernel(cells, count, place, atoms, positions, out, *, sources, rbf):
    step = CUTOFF / (rbf - 1)
    sharp = 1.0 / step**2
    middle = rbf // 2
    slope = 2.0 * sharp * step
    shrink = math.exp(-2.0 * sharp * step * step)
    row_lane = lax.broadcasted_iota(jnp.int32, (CL, CL), 1)
    row_sub = lax.broadcasted_iota(jnp.int32, (CL, CL), 0)

    def pair(slot, carry):
        cell = cells[slot]
        target = lax.div(cell, sources)
        source = place[1] * sources + cell - target * sources
        target = place[0] * CPR + target
        at_target = pl.ds(pl.multiple_of(target * CL, CL), CL)
        at_source = pl.ds(pl.multiple_of(source * CL, CL), CL)
        squared = jnp.zeros((CL, CL), jnp.float32)
        for component in range(3):
            across = jnp.broadcast_to(positions[component : component + 1, at_target], (CL, CL))
            along = positions[component : component + 1, at_source]
            difference = jnp.transpose(across) - along
            squared = squared + difference * difference
        distance = jnp.sqrt(squared)
        itself = (row_sub == row_lane) & (target == source)
        allowed = (row_lane < atoms[source]) & (distance < CUTOFF) & jnp.logical_not(itself)
        smooth = 0.5 * (jnp.cos(math.pi / CUTOFF * distance) + 1.0)
        envelope = jnp.where(allowed, smooth, 0.0)
        inside = jnp.minimum(distance, CUTOFF)
        offset = inside - middle * step
        start = jnp.exp(-sharp * offset * offset) * envelope
        out[slot, middle * CL : (middle + 1) * CL, :] = start.astype(out.dtype)
        value, ratio = start, jnp.exp(slope * offset - sharp * step * step)
        for k in range(middle + 1, rbf):
            value = value * ratio
            out[slot, k * CL : (k + 1) * CL, :] = value.astype(out.dtype)
            ratio = ratio * shrink
        value, ratio = start, jnp.exp(-slope * offset - sharp * step * step)
        for k in range(middle - 1, -1, -1):
            value = value * ratio
            out[slot, k * CL : (k + 1) * CL, :] = value.astype(out.dtype)
            ratio = ratio * shrink
        return carry

    lax.fori_loop(0, count[0], pair, 0)


def basis_of(cells, count, place, atoms, positions, sources, rbf):
    return pl.pallas_call(
        functools.partial(basis_kernel, sources=sources, rbf=rbf),
        out_shape=jax.ShapeDtypeStruct((cells.shape[0], rbf * CL, CL), jnp.bfloat16),
        in_specs=[SMEM, SMEM, SMEM, SMEM, VMEM],
        out_specs=VMEM,
        compiler_params=pltpu.CompilerParams(vmem_limit_bytes=10 * MIB),
        name="pair_basis",
    )(cells, count, place, atoms, positions)


def message_kernel(
    cells, count, place, basis, basis_filter, *rest, sources, group, own_rows, sizes, layout
):
    row_total, col_total, rbf = layout
    outs = 2 * len(sizes)
    pieces, results, (rows, total) = rest[: -2 - outs], rest[-2 - outs : -2], rest[-2:]
    row_outer, row_inner = lax.div(place[0], 2), lax.rem(place[0], 2)
    col_outer, col_inner = lax.div(place[1], 2), lax.rem(place[1], 2)
    depth = pieces[0].shape[0]
    steps = row_total // 2
    for n, piece in enumerate(pieces):
        origin = lax.rem(row_outer + steps - n % steps, steps) * 2
        origin = origin + (row_inner if n < steps else 1 - row_inner)
        rows[pl.ds(pl.multiple_of(origin * depth, 16), depth), :] = piece[...]
    total[...] = jnp.zeros_like(total)
    unit = min(own_rows, CL)

    def first_row(number):
        owner = lax.div(number * unit, own_rows)
        ahead = lax.rem(lax.div(owner, 2) + col_total // 2 - col_outer, col_total // 2)
        first = jnp.where(lax.rem(owner, 2) == col_inner, len(group) * own_rows, 0)
        first = first + number * unit - owner * own_rows
        found = jnp.int32(-1)
        for n, by in enumerate(group):
            found = jnp.where(ahead == by, first + n * own_rows, found)
        return found

    def pair(slot, carry):
        cell = cells[slot]
        target = lax.div(cell, sources)
        source = cell - target * sources
        places = [first_row(target * (CL // unit) + n) for n in range(CL // unit)]

        @pl.when(functools.reduce(jnp.maximum, places) >= 0)
        def _():
            there = pl.ds(pl.multiple_of(source * CL, CL), CL)
            projected = rows[there, :].astype(jnp.float32)
            scaled = jnp.concatenate(
                [
                    (basis_filter[k : k + 1, :] * projected).astype(jnp.bfloat16)
                    for k in range(rbf)
                ],
                axis=0,
            )
            weights = jnp.concatenate(
                [basis[slot, k * CL : (k + 1) * CL, :] for k in range(rbf)], axis=1
            )
            found = jnp.dot(weights, scaled, preferred_element_type=jnp.float32)
            for n, first in enumerate(places):

                @pl.when(first >= 0)
                def _():
                    at = pl.ds(pl.multiple_of(first, unit), unit)
                    total[at, :] += found[n * unit : (n + 1) * unit]

        return carry

    lax.fori_loop(0, count[0], pair, 0)
    first = 0
    for result in results:
        result[...] = total[first : first + result.shape[0], :].astype(result.dtype)
        first += result.shape[0]


def messages_of(cells, count, place, basis, basis_filter, pieces, sources, group, own_rows, sizes, totals):
    channels = pieces[0].shape[1]
    layout = (*totals, basis_filter.shape[0])
    results = pl.pallas_call(
        functools.partial(
            message_kernel,
            sources=sources,
            group=group,
            own_rows=own_rows,
            sizes=sizes,
            layout=layout,
        ),
        out_shape=[jax.ShapeDtypeStruct((n, channels), jnp.bfloat16) for n in sizes]
        + [jax.ShapeDtypeStruct((n, channels), jnp.float32) for n in sizes],
        in_specs=[SMEM] * 3 + [VMEM] * (2 + len(pieces)),
        out_specs=[VMEM] * (2 * len(sizes)),
        scratch_shapes=[
            pltpu.VMEM((sources * CL, channels), jnp.bfloat16),
            pltpu.VMEM((2 * len(group) * own_rows, channels), jnp.float32),
        ],
        compiler_params=pltpu.CompilerParams(vmem_limit_bytes=16 * MIB),
        name="pair_messages",
    )(cells, count, place, basis, basis_filter, *pieces)
    return results[: len(sizes)], results[len(sizes) :]


def add_kernel(kept, received, out):
    out[...] = (kept[...] + received[...].astype(jnp.float32)).astype(out.dtype)


def add_received(kept, received):
    return pl.pallas_call(
        add_kernel,
        out_shape=jax.ShapeDtypeStruct(kept.shape, jnp.bfloat16),
        in_specs=[VMEM, VMEM],
        out_specs=VMEM,
        compiler_params=pltpu.CompilerParams(vmem_limit_bytes=4 * MIB),
        name="add_received",
    )(kept, received)


def refine_kernel(
    place, atoms, hidden_weight, hidden_bias, output_weight, output_bias, kept, *rest
):
    far, parts, (out, upper, lower, message) = rest[:2], rest[2:-4], rest[-4:]
    total = kept[...]
    for part in parts:
        total = total + part[...].astype(jnp.float32)
    message[...] = total
    cut = upper.shape[0]
    message[:cut, :] += far[0][...].astype(jnp.float32)
    message[cut:, :] += far[1][...].astype(jnp.float32)
    rounded = message[...].astype(jnp.bfloat16)
    hidden = jnp.dot(rounded, hidden_weight[...], preferred_element_type=jnp.float32)
    hidden = hidden + hidden_bias[...]
    soft = jnp.maximum(hidden, 0.0) + jnp.log1p(jnp.exp(-jnp.abs(hidden)))
    hidden = (soft - math.log(2.0)).astype(jnp.bfloat16)
    result = jnp.dot(hidden, output_weight[...], preferred_element_type=jnp.float32)
    result = result + output_bias[...]
    unit = min(out.shape[0], CL)
    for n in range(out.shape[0] // unit):
        at = slice(n * unit, (n + 1) * unit)
        atom = place[0] * (CPR * CL) + place[1] * out.shape[0] + n * unit
        valid = atoms[lax.div(atom, CL)] - lax.rem(atom, CL)
        keeping = lax.broadcasted_iota(jnp.int32, (unit, out.shape[1]), 0) < valid
        out[at, :] = jnp.where(keeping, result[at, :], 0.0).astype(out.dtype)
    upper[...] = out[:cut, :]
    lower[...] = out[cut:, :]


def refine(
    place, atoms, hidden_weight, hidden_bias, output_weight, output_bias, kept, far, parts
):
    rows, channels = kept.shape
    return pl.pallas_call(
        refine_kernel,
        out_shape=[
            jax.ShapeDtypeStruct((n, channels), jnp.bfloat16) for n in (rows, rows // 2, rows // 2)
        ],
        in_specs=[SMEM] * 2 + [VMEM] * (7 + len(parts)),
        out_specs=[VMEM] * 3,
        scratch_shapes=[pltpu.VMEM(kept.shape, jnp.float32)],
        compiler_params=pltpu.CompilerParams(vmem_limit_bytes=10 * MIB),
        name="update_rows",
    )(
        place,
        atoms,
        hidden_weight,
        hidden_bias[None],
        output_weight,
        output_bias[None],
        kept,
        *far,
        *parts,
    )


def local(
    features,
    positions,
    cluster_atoms,
    pair_cells,
    pair_count,
    project_weight,
    basis_filter,
    hidden_weight,
    hidden_bias,
    output_weight,
    output_bias,
):
    row_total, col_total = lax.axis_size("row"), lax.axis_size("col")
    row_index, col_index = lax.axis_index("row"), lax.axis_index("col")
    row_outer, col_outer = row_total // 2, col_total // 2
    sources = features.shape[0] * row_total // CL
    own_rows = CPR * CL // col_total
    rbf = basis_filter.shape[0]

    def shift(value, axis, total, by):
        outer = total // 2
        pairs = [(2 * o + i, 2 * ((o + by) % outer) + i) for o in range(outer) for i in range(2)]
        return lax.ppermute(value, axis, pairs)

    def swap(value, axis, total):
        return lax.ppermute(value, axis, [(n, n ^ 1) for n in range(total)])

    cells, count = pair_cells[0, 0], pair_count[0]
    place = jnp.stack([row_index, col_index]).astype(jnp.int32)

    projected = jnp.dot(features, project_weight, preferred_element_type=jnp.float32)
    projected = projected.astype(jnp.bfloat16)
    near = [projected] + [shift(projected, "row", row_total, by) for by in range(1, row_outer)]
    basis = basis_of(cells, count, place, cluster_atoms, positions, sources, rbf)
    basis, *near[1:] = lax.optimization_barrier((basis, *near[1:]))
    far = [swap(piece, "row", row_total) for piece in near]
    pieces = near + far

    half = col_outer // 2
    others = [by for by in range(1, col_outer) if by != half]
    cut = own_rows // 2

    def group_messages(cells, group, sizes):
        return messages_of(
            cells, count, place, basis, basis_filter, pieces, sources, group, own_rows, sizes,
            (row_total, col_total),
        )

    send, keep = group_messages(cells, [half], [cut, cut])
    received = [swap(s, "col", col_total) for s in send]
    far_sums = [add_received(k, r) for k, r in zip(keep, received)]
    far_parts = [shift(part, "col", col_total, half) for part in far_sums]
    cells, *_ = lax.optimization_barrier((cells, *send))
    send, keep = group_messages(cells, others, [own_rows] * len(others))
    received = [swap(s, "col", col_total) for s in send]
    other_sums = [add_received(k, r) for k, r in zip(keep, received)]
    other_parts = [shift(part, "col", col_total, by) for part, by in zip(other_sums, others)]
    cells, *_ = lax.optimization_barrier((cells, *send, *far_sums))
    (send,), (keep,) = group_messages(cells, [0], [own_rows])
    arrived = [swap(send, "col", col_total)] + other_parts

    mine = refine(
        place, cluster_atoms, hidden_weight, hidden_bias, output_weight, output_bias, keep,
        far_parts, arrived,
    )
    whole, halves = mine[0], mine[1:]

    found = {(0, 0): [whole], (0, 1): [swap(whole, "col", col_total)]}
    for by in others:
        found[by, 0] = [shift(whole, "col", col_total, by)]
    *halves, _ = lax.optimization_barrier((*halves, found[0, 1][0]))
    found[half, 0] = [shift(part, "col", col_total, half) for part in halves]
    for by in others + [half]:
        found[by, 1] = [swap(part, "col", col_total) for part in found[by, 0]]
    result = jnp.zeros((CPR * CL, whole.shape[1]), whole.dtype)
    col_o, col_i = col_index // 2, col_index % 2
    for (by, other), parts in found.items():
        from_o = (col_o - by) % col_outer
        from_i = 1 - col_i if other else col_i
        first = (from_o * 2 + from_i) * own_rows
        for part in parts:
            result = lax.dynamic_update_slice_in_dim(result, part, first, 0)
            first = first + part.shape[0]
    return result


def solution(mesh):
    in_specs = (
        P(("col", "row"), None),
        P(),
        P(),
        P("row", "col", None),
        P("row", "col"),
        P(),
        P(),
        P(),
        P(),
        P(),
        P(),
    )
    out_specs = P("row", None)
    return jax.shard_map(local, mesh=mesh, in_specs=in_specs, out_specs=out_specs, check_vma=False)
```
